32 devices in a mesh: groups: 2 (over y), coef: 4 (over x, core), slab: 4 (over z).
Axes of the slice: x: 2, y: 2, z: 4, core: 2. Of those that a mesh axis runs over, the one named last changes fastest.
Arguments:
- coefficients: float32 [896, 32768], P('coef', ('groups', 'slab')), parts along dimension 1, may hold values from -6 to 6
- measured: float32 [16, 4, 64, 256], P('groups', 'slab'), parts along dimension 0, may hold values from -6 to 6
- ray_voxels: int32 [8, 64, 128], replicated, may hold values from 0 to 4095
- ray_weights: int32 [8, 64, 128], replicated, may hold values from 1 to 63
- angle_ids: int32 [8], replicated, may hold values from 0 to 15
- angle_table: bfloat16 [16, 896, 256], P(None, 'coef'), may hold values from -0.1875 to 0.1875
- harmonics: bfloat16 [896, 2048], P('coef'), may hold values from -0.1875 to 0.1875
Outputs:
- updated: float32 [896, 32768], P('coef', ('groups', 'slab')), parts along dimension 1
- residual: float32 [16, 4, 64, 256], P('groups', 'slab', None, 'coef'), parts along dimension 0
The draws below stay inside these ranges and needn't reach their ends.
There are 2 independent parts, one for each index of `groups`. The reference program is written for one: setup_inputs(seed, part) draws one part's arguments, and reference() takes and returns one part's arrays. A program takes and returns all parts, laid end to end along the dimension named above; an argument that names none is the same for every part. Nothing has to cross between parts.
All inputs are finite; a program needn't handle non-finite values.
Results may differ from the reference program's by a relative error of at most 0.0034.
Values may be sent and summed in bfloat16 or wider, within the bound.
A program may use at most 64 MiB of HBM per device.

```python
import jax
import jax.numpy as jnp
from jax import lax

NG = 64
P_SIZE = 8
NA = 16
HARMONIC_COUNT = 896
CH = 256
O = 2048
SAMPLES = 128
NZ = 4
VOXEL_TOTAL = 16384


def set_ends(values, own_key, smallest, largest):
    place = [jax.random.randint(jax.random.fold_in(own_key, axis), (), 0, length) for axis, length in enumerate(values.shape)]
    main_axis = values.shape.index(max(values.shape))
    neighbour = place[:main_axis] + [(place[main_axis] + 1) % values.shape[main_axis]] + place[main_axis + 1:]
    return values.at[tuple(place)].set(smallest).at[tuple(neighbour)].set(largest)


def level_of(stream_key, dims, cuts, least, top_value):
    def one(axis_at, blocks):
        steps = jax.random.uniform(jax.random.fold_in(jax.random.fold_in(stream_key, 6), axis_at), (blocks,), jnp.float32, least / len(cuts), top_value / len(cuts))
        return jnp.repeat(jnp.exp(steps), dims[axis_at] // blocks).reshape((-1,) + (1,) * (len(dims) - axis_at - 1))

    gain = one(*cuts[0])
    for cut in cuts[1:]:
        gain = gain * one(*cut)
    return gain


def noise(stream_key, dims, deviation, limit, split=(), dtype=jnp.bfloat16):
    array = jax.random.normal(stream_key, dims, jnp.float32) * deviation
    if len(split) > 0:
        array = level_of(stream_key, dims, split, -0.22, 0.18) * array
    return jnp.clip(array, min=-limit, max=limit).astype(dtype)


def setup_inputs(seed: int = 0, part: int = 0) -> dict:
    arg_keys = jax.random.split(jax.random.key(seed), 8)
    own_keys = jax.random.split(jax.random.fold_in(arg_keys[7], part), 8)
    return {
        "coefficients": noise(own_keys[0], (HARMONIC_COUNT, VOXEL_TOTAL), 1.0, 6.0, ((0, 4), (1, 4)), jnp.float32),
        "measured": noise(own_keys[1], (P_SIZE, NZ, NG, CH), 1.0, 6.0, ((1, 4),), jnp.float32),
        "ray_voxels": set_ends(jax.random.randint(arg_keys[2], (P_SIZE, NG, SAMPLES), 0, NG * NG), jax.random.fold_in(arg_keys[2], 1), 0, (NG * NG) - 1).astype(jnp.int32),
        "ray_weights": set_ends(jax.random.randint(arg_keys[3], (P_SIZE, NG, SAMPLES), 1, 64), jax.random.fold_in(arg_keys[3], 1), 1, 63).astype(jnp.int32),
        "angle_ids": set_ends(jax.random.randint(arg_keys[4], (P_SIZE,), 0, NA), jax.random.fold_in(arg_keys[4], 1), 0, NA - 1).astype(jnp.int32),
        "angle_table": noise(arg_keys[5], (NA, HARMONIC_COUNT, CH), HARMONIC_COUNT ** -0.5, 0.1875, ((1, 4),)),
        "harmonics": noise(arg_keys[6], (HARMONIC_COUNT, O), HARMONIC_COUNT ** -0.5, 0.1875, ((0, 4),)),
    }


def build_matrix(ray_voxels, ray_weights):
    shape_all = ray_voxels.shape
    angle_pos = jnp.broadcast_to(jnp.arange(shape_all[0])[:, None, None], shape_all)
    ray_pos = jnp.broadcast_to(jnp.arange(shape_all[1])[None, :, None], shape_all)
    values = ray_weights.astype(jnp.float32) / 256.0
    system_matrix = jnp.zeros((shape_all[0], shape_all[1], NG * NG), jnp.float32).at[angle_pos, ray_pos, ray_voxels].add(values)
    return system_matrix.astype(jnp.bfloat16)


def select_angles(angle_ids, angle_table):
    entries = angle_table.shape[0]
    onehot = (angle_ids[:, None] == jnp.arange(entries)[None, :]).astype(jnp.bfloat16)
    flat_table = angle_table.reshape(entries, -1)
    picked = jnp.dot(onehot, flat_table, preferred_element_type=jnp.float32)
    return picked.astype(jnp.bfloat16).reshape((angle_ids.shape[0],) + angle_table.shape[1:])


def reference(coefficients, measured, ray_voxels, ray_weights, angle_ids, angle_table, harmonics):
    system_matrix = build_matrix(ray_voxels, ray_weights).astype(jnp.float32)
    chosen = select_angles(angle_ids, angle_table).astype(jnp.float32)
    coef_half = coefficients.astype(jnp.bfloat16)
    stacked_rows = coef_half.astype(jnp.float32).reshape(HARMONIC_COUNT, NZ, NG * NG)
    ray_totals = jnp.einsum('dmj,hqj->dqmh', system_matrix, stacked_rows).astype(jnp.bfloat16)
    ray_totals = lax.optimization_barrier(ray_totals).astype(jnp.float32)
    predicted = jnp.einsum('azrk,akc->azrc', ray_totals, chosen)
    residual = predicted - measured
    resid_half = lax.optimization_barrier(residual.astype(jnp.bfloat16)).astype(jnp.float32)
    backward_projection = jnp.einsum('azrc,akc->azrk', resid_half, chosen).astype(jnp.bfloat16)
    backward_projection = lax.optimization_barrier(backward_projection).astype(jnp.float32)
    misfit_gradient = jnp.einsum('qci,qbcy->ybi', system_matrix, backward_projection).reshape(HARMONIC_COUNT, VOXEL_TOTAL)

    def regular_layer(layer_coef):
        orient_field = lax.dot_general(layer_coef, harmonics, (((0,), (0,)), ((), ())), preferred_element_type=jnp.float32)
        slope_half = (-jax.nn.sigmoid(-orient_field)).astype(jnp.bfloat16)
        return lax.dot_general(harmonics, slope_half, (((1,), (1,)), ((), ())), preferred_element_type=jnp.float32)

    by_layer = jnp.transpose(coef_half.reshape(HARMONIC_COUNT, NZ, NG * NG), (1, 0, 2))
    reg_layers = lax.map(regular_layer, by_layer)
    reg_grad = jnp.transpose(reg_layers, (1, 0, 2)).reshape(HARMONIC_COUNT, VOXEL_TOTAL)
    updated = coefficients - 0.5 * misfit_gradient - 0.5 * reg_grad
    return updated, residual
```

```python
import functools

import jax
import jax.numpy as jnp
from jax import lax
from jax.experimental import pallas as pl
from jax.experimental.pallas import tpu as pltpu
from jax.sharding import PartitionSpec as P

NG = 64
LANES = 128
BF = jnp.bfloat16
F32 = jnp.float32
NT = (((1,), (1,)), ((), ()))
TN = (((0,), (0,)), ((), ()))
NN = (((1,), (0,)), ((), ()))


def dot(a, b, dims):
    return lax.dot_general(a, b, dims, preferred_element_type=F32)


def kernel(n, tiles, coef_hbm, meas_hbm, vox_ref, wgt_ref, ids_ref, table_hbm, harm_hbm,
           upd_hbm, resid_ref,
           coef, coef_bf, meas, table, harm, recv, matrix, prod, rays, ray_acc, parts, inbox,
           bp_t, racc, rsend, rrecv,
           load_sem, out_sem, hsend, hrecv, csend, crecv, psend, precv, gsend, grecv):
    me = lax.axis_index("coef")
    cl, width = coef.shape
    share = width // n
    vt = share // tiles
    angles, layers, nrays, chans = meas.shape
    plane = NG * NG
    orient = harm.shape[2]
    steps = n.bit_length() - 1
    sibling = me + 1 - 2 * lax.rem(me, 2)

    loads = [
        pltpu.make_async_copy(coef_hbm, coef, load_sem.at[0]),
        pltpu.make_async_copy(harm_hbm, harm.at[me], load_sem.at[1]),
        pltpu.make_async_copy(table_hbm, table, load_sem.at[2]),
        pltpu.make_async_copy(meas_hbm, meas, load_sem.at[3]),
    ]
    for item in loads:
        item.start()

    barrier = pltpu.get_barrier_semaphore()
    for d in range(1, n):
        pl.semaphore_signal(barrier, inc=1, device_id={"coef": lax.rem(me + d, n)},
                            device_id_type=pl.DeviceIdType.MESH)
    pl.semaphore_wait(barrier, n - 1)

    def remote(src, dst, ssem, rsem, target):
        return pltpu.make_async_remote_copy(
            src_ref=src, dst_ref=dst, send_sem=ssem, recv_sem=rsem,
            device_id={"coef": target}, device_id_type=pl.DeviceIdType.MESH)

    harm_direct = []
    for e in range(1, n // 2):
        harm_direct.append(remote(harm_hbm, harm.at[me], hsend.at[0, e], hrecv.at[me],
                                  lax.rem(me + 2 * e, n)))
        harm_direct[-1].start()
    harm_sib = remote(harm_hbm, harm.at[me], hsend.at[0, 0], hrecv.at[me], sibling)
    harm_sib.start()

    loads[0].wait()
    coef_copies = []
    for t in range(tiles):
        for d in range(n):
            j = lax.rem(me + d, n)
            at = pl.multiple_of(j * share + t * vt, LANES)
            block = coef[:, pl.ds(at, vt)].astype(BF)
            coef_bf[:, pl.ds(at, vt)] = block
            if d == 0:
                recv[t, me] = block
    for t in range(tiles):
        for d in range(1, n):
            j = lax.rem(me + d, n)
            at = pl.multiple_of(j * share + t * vt, LANES)
            item = remote(coef_bf.at[:, pl.ds(at, vt)], recv.at[t, me], csend.at[t, d],
                          crecv.at[t, me], j)
            item.start()
            coef_copies.append(item)

    samples = vox_ref.shape[1]
    rows_hi = plane // LANES
    pos_lo = lax.broadcasted_iota(jnp.int32, (LANES, samples), 0)
    pos_hi = lax.broadcasted_iota(jnp.int32, (rows_hi, samples), 0)

    def build(g, carry):
        r0 = pl.multiple_of(g * 16, 16)
        vox = vox_ref[pl.ds(r0, 16), :]
        wgt = wgt_ref[pl.ds(r0, 16), :].astype(F32) * (1.0 / 256.0)
        high = vox // LANES
        low = vox - high * LANES
        for i in range(16):
            oh_hi = jnp.where(high[i:i + 1, :] == pos_hi, wgt[i:i + 1, :], 0.0).astype(BF)
            oh_lo = jnp.where(low[i:i + 1, :] == pos_lo, 1.0, 0.0).astype(BF)
            prod[pl.ds(i * rows_hi, rows_hi), :] = dot(oh_hi, oh_lo, NT)
        for h in range(rows_hi):
            matrix[pl.ds(r0, 16), pl.ds(h * LANES, LANES)] = prod[
                pl.ds(h, 16, stride=rows_hi), :].astype(BF)
        return carry

    lax.fori_loop(0, (angles * nrays) // 16, build, 0)

    kc = 512
    loads[2].wait()
    for z in range(layers):
        ray_acc[...] = jnp.zeros_like(ray_acc)

        def project(i, carry, z=z):
            at = pl.multiple_of(i * kc, kc)
            ray_acc[...] += dot(matrix[:, pl.ds(at, kc)],
                                coef_bf[:, pl.ds(pl.multiple_of(z * plane + i * kc, kc), kc)], NT)
            return carry

        lax.fori_loop(0, plane // kc, project, 0)
        rays[...] = ray_acc[...].astype(BF)
        for a in range(angles):
            parts[0, a, z] = dot(rays[a * nrays:(a + 1) * nrays, :], table[ids_ref[a]], NN)

    def swap(s):
        bit = 1 << s
        partner = me + (1 - 2 * lax.rem(me // bit, 2)) * bit
        return remote(parts.at[s], inbox.at[s], psend.at[s], precv.at[s], partner)

    swaps = [swap(s) for s in range(steps)]
    swaps[0].start()

    loads[1].wait()
    forwards = []
    for e in range(1, n // 2):
        j = lax.rem(me + 2 * e, n)
        remote(harm_hbm, harm.at[j], hsend.at[0, e], hrecv.at[j], j).wait_recv()
        item = remote(harm.at[j], harm.at[j], hsend.at[1, e], hrecv.at[j], sibling)
        item.start()
        forwards.append(item)
    for e in range(n // 2):
        j = lax.rem(sibling + 2 * e, n)
        remote(harm.at[j], harm.at[j], hsend.at[1, 0], hrecv.at[j], sibling).wait_recv()

    def finish_swap(s):
        swaps[s].wait()
        parts[s + 1] = parts[s] + inbox[s]
        if s + 1 < steps:
            swaps[s + 1].start()

    oc = 512
    back = []
    done_swaps = 0
    for t in range(tiles):
        for d in range(1, n):
            j = lax.rem(me + d, n)
            remote(coef_bf.at[:, pl.ds(0, vt)], recv.at[t, j], csend.at[t, d],
                   crecv.at[t, j], j).wait_recv()
        racc[...] = jnp.zeros_like(racc)

        def penalty(i, carry, t=t):
            at = pl.multiple_of(i * oc, oc)
            field = dot(harm[0, :, pl.ds(at, oc)], recv[t, 0], TN)
            for j in range(1, n):
                field += dot(harm[j, :, pl.ds(at, oc)], recv[t, j], TN)
            slope = (-1.0 / (1.0 + jnp.exp(field))).astype(BF)
            for j in range(n):
                racc[j] += dot(harm[j, :, pl.ds(at, oc)], slope, NN)
            return carry

        lax.fori_loop(0, orient // oc, penalty, 0)
        if done_swaps < steps:
            finish_swap(done_swaps)
            done_swaps += 1
        rsend[t] = racc[...].astype(BF)
        rrecv[t, me] = rsend[t, me]
        for d in range(1, n):
            j = lax.rem(me + d, n)
            item = remote(rsend.at[t, j], rrecv.at[t, me], gsend.at[t, d], grecv.at[t, me], j)
            item.start()
            back.append(item)
    while done_swaps < steps:
        finish_swap(done_swaps)
        done_swaps += 1

    loads[3].wait()
    resid_ref[...] = parts[steps] - meas[...]
    for z in range(layers):
        for a in range(angles):
            bp_t[:, a * nrays:(a + 1) * nrays] = dot(
                table[ids_ref[a]], resid_ref[a, z].astype(BF), NT).astype(BF)

        def gradient(i, carry, z=z):
            at = pl.multiple_of(i * kc, kc)
            to = pl.multiple_of(z * plane + i * kc, kc)
            coef[:, pl.ds(to, kc)] = coef[:, pl.ds(to, kc)] - 0.5 * dot(
                bp_t[...], matrix[:, pl.ds(at, kc)], NN)
            return carry

        lax.fori_loop(0, plane // kc, gradient, 0)

    outs = []
    for t in range(tiles):
        for d in range(n):
            j = lax.rem(me + d, n)
            if d > 0:
                remote(rsend.at[t, j], rrecv.at[t, j], gsend.at[t, d], grecv.at[t, j], j).wait_recv()
            at = pl.multiple_of(j * share + t * vt, LANES)
            coef[:, pl.ds(at, vt)] = coef[:, pl.ds(at, vt)] - 0.5 * rrecv[t, j].astype(F32)
            item = pltpu.make_async_copy(coef.at[:, pl.ds(at, vt)], upd_hbm.at[:, pl.ds(at, vt)],
                                         out_sem.at[t, d])
            item.start()
            outs.append(item)
    for item in harm_direct + [harm_sib] + forwards + coef_copies + back:
        item.wait_send()
    for item in outs:
        item.wait()


def body(coefficients, measured, ray_voxels, ray_weights, angle_ids, angle_table, harmonics):
    n = lax.axis_size("coef")
    cl, width = coefficients.shape
    angles, layers, nrays, chans = measured.shape
    rows = angles * nrays
    orient = harmonics.shape[1]
    share = width // n
    tiles = 2
    vt = share // tiles
    steps = n.bit_length() - 1
    any_spec = pl.BlockSpec(memory_space=pl.ANY)
    vmem_spec = pl.BlockSpec(memory_space=pltpu.VMEM)
    smem_spec = pl.BlockSpec(memory_space=pltpu.SMEM)
    dma = pltpu.SemaphoreType.DMA
    updated, residual = pl.pallas_call(
        functools.partial(kernel, n, tiles),
        out_shape=(jax.ShapeDtypeStruct(coefficients.shape, F32),
                   jax.ShapeDtypeStruct(measured.shape, F32)),
        in_specs=[any_spec, any_spec, vmem_spec, vmem_spec, smem_spec, any_spec, any_spec],
        out_specs=(any_spec, vmem_spec),
        scratch_shapes=[
            pltpu.VMEM((cl, width), F32),
            pltpu.VMEM((cl, width), BF),
            pltpu.VMEM(measured.shape, F32),
            pltpu.VMEM(angle_table.shape, BF),
            pltpu.VMEM((n, cl, orient), BF),
            pltpu.VMEM((tiles, n, cl, vt), BF),
            pltpu.VMEM((rows, NG * NG), BF),
            pltpu.VMEM((16 * (NG * NG // LANES), LANES), F32),
            pltpu.VMEM((rows, cl), BF),
            pltpu.VMEM((rows, cl), F32),
            pltpu.VMEM((steps + 1,) + measured.shape, F32),
            pltpu.VMEM((steps,) + measured.shape, F32),
            pltpu.VMEM((cl, rows), BF),
            pltpu.VMEM((n, cl, vt), F32),
            pltpu.VMEM((tiles, n, cl, vt), BF),
            pltpu.VMEM((tiles, n, cl, vt), BF),
            dma((4,)),
            dma((tiles, n)),
            dma((2, n)),
            dma((n,)),
            dma((tiles, n)),
            dma((tiles, n)),
            dma((steps,)),
            dma((steps,)),
            dma((tiles, n)),
            dma((tiles, n)),
        ],
        compiler_params=pltpu.CompilerParams(
            collective_id=0, has_side_effects=True, vmem_limit_bytes=60 * 1024 * 1024),
        name="step",
    )(coefficients, measured, ray_voxels.reshape(rows, -1), ray_weights.reshape(rows, -1),
      angle_ids, angle_table, harmonics)
    chan_width = chans // n
    residual = lax.dynamic_slice_in_dim(residual, lax.axis_index("coef") * chan_width, chan_width, 3)
    return updated, residual


def solution(mesh):
    in_specs = (
        P("coef", ("groups", "slab")),
        P("groups", "slab", None, None),
        P(),
        P(),
        P(),
        P(None, "coef", None),
        P("coef", None),
    )
    out_specs = (P("coef", ("groups", "slab")), P("groups", "slab", None, "coef"))
    return jax.shard_map(body, mesh=mesh, in_specs=in_specs, out_specs=out_specs, check_vma=False)
```

```python
import functools

import jax
import jax.numpy as jnp
from jax import lax
from jax.experimental import pallas as pl
from jax.experimental.pallas import tpu as pltpu
from jax.sharding import PartitionSpec as P

NG = 64
LANES = 128
BF = jnp.bfloat16
F32 = jnp.float32
NT = (((1,), (1,)), ((), ()))
TN = (((0,), (0,)), ((), ()))
NN = (((1,), (0,)), ((), ()))


def dot(a, b, dims):
    return lax.dot_general(a, b, dims, preferred_element_type=F32)


def kernel(n, slabs, split, tiles, coef_hbm, meas_hbm, vox_ref, wgt_ref, ids_ref, table_hbm, harm_hbm,
           upd_hbm, resid_ref,
           coef, coef_bf, meas, table, harm, recv, matrix, prod, rays, ray_acc, part, half, inbox, full,
           bp_t, racc, rsend, rrecv,
           load_sem, out_sem, own_s, own_r, hx_s, hx_r, hz_s, hz_r, hy_s, hy_r, hs_s, hs_r,
           csend, crecv, psend, precv, gsend, grecv):
    me = lax.axis_index("coef")
    mz = lax.axis_index("slab")
    my = lax.axis_index("groups") if split > 1 else 0
    cl, width = coef.shape
    share = width // n
    vt = share // tiles
    angles, layers, nrays, chans = meas.shape
    plane = NG * NG
    orient = harm.shape[2]
    steps = n.bit_length() - 1
    sibling = me + 1 - 2 * lax.rem(me, 2)

    loads = [
        pltpu.make_async_copy(coef_hbm, coef, load_sem.at[0]),
        pltpu.make_async_copy(harm_hbm, harm.at[me], load_sem.at[1]),
        pltpu.make_async_copy(table_hbm, table, load_sem.at[2]),
        pltpu.make_async_copy(meas_hbm, meas, load_sem.at[3]),
    ]
    for item in loads:
        item.start()

    barrier = pltpu.get_barrier_semaphore()
    for axis, index, size in (("coef", me, n), ("slab", mz, slabs), ("groups", my, split)):
        for d in range(1, size):
            pl.semaphore_signal(barrier, inc=1, device_id={axis: lax.rem(index + d, size)},
                                device_id_type=pl.DeviceIdType.MESH)
    pl.semaphore_wait(barrier, n + slabs + split - 3)

    def remote(src, dst, ssem, rsem, target, axis="coef"):
        return pltpu.make_async_remote_copy(
            src_ref=src, dst_ref=dst, send_sem=ssem, recv_sem=rsem,
            device_id={axis: target}, device_id_type=pl.DeviceIdType.MESH)

    ow = orient // (slabs * split)
    mates = [lax.rem(me + 2 * e, n) for e in range(1, n // 2)]
    sib_mates = [lax.rem(sibling + 2 * e, n) for e in range(1, n // 2)]
    sent = []

    def cols(zi, yi):
        return pl.ds(pl.multiple_of((zi * split + yi) * ow, LANES), ow)

    def launch(*args):
        item = remote(*args)
        item.start()
        sent.append(item)

    def arrived(ref, sem):
        remote(ref, ref, sem, sem, sibling).wait_recv()

    def spread_y(b, zi):
        piece = harm.at[b, :, cols(zi, my)]
        for d in range(1, split):
            to = lax.rem(my + d, split)
            launch(piece, piece, hy_s.at[b, zi, to], hy_r.at[b, zi, my], to, "groups")

    def to_sibling(b, zi, yi):
        piece = harm.at[b, :, cols(zi, yi)]
        launch(piece, piece, hs_s.at[b, zi, yi], hs_r.at[b, zi, yi], sibling)

    for b in mates:
        launch(harm_hbm.at[:, cols(mz, my)], harm.at[me, :, cols(mz, my)], hx_s.at[b],
               hx_r.at[me], b)
    launch(harm_hbm, harm.at[me], own_s.at[0], own_r.at[0], sibling)

    def x_arrive():
        for b in mates:
            piece = harm.at[b, :, cols(mz, my)]
            arrived(piece, hx_r.at[b])
            for d in range(1, slabs):
                to = lax.rem(mz + d, slabs)
                launch(piece, piece, hz_s.at[b, to], hz_r.at[b, mz], to, "slab")
            spread_y(b, mz)
            to_sibling(b, mz, my)

    def z_arrive(d):
        zi = lax.rem(mz + d, slabs)
        for b in mates:
            arrived(harm.at[b, :, cols(zi, my)], hz_r.at[b, zi])
            spread_y(b, zi)
            to_sibling(b, zi, my)

    def y_arrive():
        for d in range(slabs):
            zi = lax.rem(mz + d, slabs)
            for b in mates:
                for f in range(1, split):
                    yi = lax.rem(my + f, split)
                    arrived(harm.at[b, :, cols(zi, yi)], hy_r.at[b, zi, yi])
                    to_sibling(b, zi, yi)

    def sibling_arrive():
        arrived(harm.at[sibling], own_r.at[0])
        for b in sib_mates:
            for zi in range(slabs):
                for yi in range(split):
                    arrived(harm.at[b, :, cols(zi, yi)], hs_r.at[b, zi, yi])

    loads[0].wait()
    coef_copies = []
    for t in range(tiles):
        for d in range(n):
            j = lax.rem(me + d, n)
            at = pl.multiple_of(j * share + t * vt, LANES)
            block = coef[:, pl.ds(at, vt)].astype(BF)
            coef_bf[:, pl.ds(at, vt)] = block
            if d == 0:
                recv[t, me] = block
    for t in range(tiles):
        for d in range(1, n):
            j = lax.rem(me + d, n)
            at = pl.multiple_of(j * share + t * vt, LANES)
            item = remote(coef_bf.at[:, pl.ds(at, vt)], recv.at[t, me], csend.at[t, d],
                          crecv.at[t, me], j)
            item.start()
            coef_copies.append(item)

    samples = vox_ref.shape[1]
    rows_hi = plane // LANES
    pos_lo = lax.broadcasted_iota(jnp.int32, (LANES, samples), 0)
    pos_hi = lax.broadcasted_iota(jnp.int32, (rows_hi, samples), 0)

    def build(g, carry):
        r0 = pl.multiple_of(g * 16, 16)
        vox = vox_ref[pl.ds(r0, 16), :]
        wgt = wgt_ref[pl.ds(r0, 16), :].astype(F32) * (1.0 / 256.0)
        high = vox // LANES
        low = vox - high * LANES
        for i in range(16):
            oh_hi = jnp.where(high[i:i + 1, :] == pos_hi, wgt[i:i + 1, :], 0.0).astype(BF)
            oh_lo = jnp.where(low[i:i + 1, :] == pos_lo, 1.0, 0.0).astype(BF)
            prod[pl.ds(i * rows_hi, rows_hi), :] = dot(oh_hi, oh_lo, NT)
        for h in range(rows_hi):
            matrix[pl.ds(r0, 16), pl.ds(h * LANES, LANES)] = prod[
                pl.ds(h, 16, stride=rows_hi), :].astype(BF)
        return carry

    groups16 = (angles * nrays) // 16
    parts = 4
    for q in range(parts):
        lax.fori_loop(q * groups16 // parts, (q + 1) * groups16 // parts, build, 0)
        if q == 0:
            x_arrive()
        elif q < slabs:
            z_arrive(q)
    for q in range(parts, slabs):
        z_arrive(q)

    kc = 512
    loads[2].wait()
    for z in range(layers):
        ray_acc[...] = jnp.zeros_like(ray_acc)

        def project(i, carry, z=z):
            at = pl.multiple_of(i * kc, kc)
            ray_acc[...] += dot(matrix[:, pl.ds(at, kc)],
                                coef_bf[:, pl.ds(pl.multiple_of(z * plane + i * kc, kc), kc)], NT)
            return carry

        lax.fori_loop(0, plane // kc, project, 0)
        rays[...] = ray_acc[...].astype(BF)
        for a in range(angles):
            part[a, z] = dot(rays[a * nrays:(a + 1) * nrays, :], table[ids_ref[a]], NN)

    ha = angles // 2
    par = lax.rem(me, 2)
    mine, other = pl.ds(par * ha, ha), pl.ds((1 - par) * ha, ha)

    def swap(s):
        if s == 0:
            return remote(part.at[other], inbox.at[0], psend.at[0], precv.at[0], sibling)
        if s == steps:
            return remote(half.at[s - 1], full.at[mine], psend.at[s], precv.at[s], sibling)
        bit = 1 << s
        partner = me + (1 - 2 * lax.rem(me // bit, 2)) * bit
        return remote(half.at[s - 1], inbox.at[s], psend.at[s], precv.at[s], partner)

    swaps = [swap(s) for s in range(steps + 1)]
    swaps[0].start()

    def finish_swap(s):
        swaps[s].wait_recv()
        if s < steps:
            half[s] = (part[mine] if s == 0 else half[s - 1]) + inbox[s]
            swaps[s + 1].start()

    loads[1].wait()
    y_arrive()
    finish_swap(0)
    sibling_arrive()

    oc = 512
    back = []
    done_swaps = 1
    for t in range(tiles):
        for d in range(1, n):
            j = lax.rem(me + d, n)
            remote(coef_bf.at[:, pl.ds(0, vt)], recv.at[t, j], csend.at[t, d],
                   crecv.at[t, j], j).wait_recv()
        racc[...] = jnp.zeros_like(racc)

        def penalty(i, carry, t=t):
            at = pl.multiple_of(i * oc, oc)
            field = dot(harm[0, :, pl.ds(at, oc)], recv[t, 0], TN)
            for j in range(1, n):
                field += dot(harm[j, :, pl.ds(at, oc)], recv[t, j], TN)
            slope = (-1.0 / (1.0 + jnp.exp(field))).astype(BF)
            for j in range(n):
                racc[j] += dot(harm[j, :, pl.ds(at, oc)], slope, NN)
            return carry

        lax.fori_loop(0, orient // oc, penalty, 0)
        rsend[t] = racc[...].astype(BF)
        rrecv[t, me] = rsend[t, me]
        for d in range(1, n):
            j = lax.rem(me + d, n)
            item = remote(rsend.at[t, j], rrecv.at[t, me], gsend.at[t, d], grecv.at[t, me], j)
            item.start()
            back.append(item)
        if done_swaps < steps:
            finish_swap(done_swaps)
            done_swaps += 1
    while done_swaps <= steps:
        finish_swap(done_swaps)
        done_swaps += 1

    loads[3].wait()
    full[mine] = half[steps - 1]
    resid_ref[...] = full[...] - meas[...]
    for z in range(layers):
        for a in range(angles):
            bp_t[:, a * nrays:(a + 1) * nrays] = dot(
                table[ids_ref[a]], resid_ref[a, z].astype(BF), NT).astype(BF)

        def gradient(i, carry, z=z):
            at = pl.multiple_of(i * kc, kc)
            to = pl.multiple_of(z * plane + i * kc, kc)
            coef[:, pl.ds(to, kc)] = coef[:, pl.ds(to, kc)] - 0.5 * dot(
                bp_t[...], matrix[:, pl.ds(at, kc)], NN)
            return carry

        lax.fori_loop(0, plane // kc, gradient, 0)

    outs = []
    for t in range(tiles):
        for d in range(n):
            j = lax.rem(me + d, n)
            if d > 0:
                remote(rsend.at[t, j], rrecv.at[t, j], gsend.at[t, d], grecv.at[t, j], j).wait_recv()
            at = pl.multiple_of(j * share + t * vt, LANES)
            coef[:, pl.ds(at, vt)] = coef[:, pl.ds(at, vt)] - 0.5 * rrecv[t, j].astype(F32)
            item = pltpu.make_async_copy(coef.at[:, pl.ds(at, vt)], upd_hbm.at[:, pl.ds(at, vt)],
                                         out_sem.at[t, d])
            item.start()
            outs.append(item)
    for item in sent + coef_copies + back + swaps:
        item.wait_send()
    for item in outs:
        item.wait()


def body(coefficients, measured, ray_voxels, ray_weights, angle_ids, angle_table, harmonics):
    n = lax.axis_size("coef")
    slabs = lax.axis_size("slab")
    split = lax.axis_size("groups")
    if (harmonics.shape[1] // (slabs * split)) % LANES:
        split = 1
    cl, width = coefficients.shape
    angles, layers, nrays, chans = measured.shape
    rows = angles * nrays
    orient = harmonics.shape[1]
    share = width // n
    tiles = 2
    vt = share // tiles
    steps = n.bit_length() - 1
    any_spec = pl.BlockSpec(memory_space=pl.ANY)
    vmem_spec = pl.BlockSpec(memory_space=pltpu.VMEM)
    smem_spec = pl.BlockSpec(memory_space=pltpu.SMEM)
    dma = pltpu.SemaphoreType.DMA
    updated, residual = pl.pallas_call(
        functools.partial(kernel, n, slabs, split, tiles),
        out_shape=(jax.ShapeDtypeStruct(coefficients.shape, F32),
                   jax.ShapeDtypeStruct(measured.shape, F32)),
        in_specs=[any_spec, any_spec, vmem_spec, vmem_spec, smem_spec, any_spec, any_spec],
        out_specs=(any_spec, vmem_spec),
        scratch_shapes=[
            pltpu.VMEM((cl, width), F32),
            pltpu.VMEM((cl, width), BF),
            pltpu.VMEM(measured.shape, F32),
            pltpu.VMEM(angle_table.shape, BF),
            pltpu.VMEM((n, cl, orient), BF),
            pltpu.VMEM((tiles, n, cl, vt), BF),
            pltpu.VMEM((rows, NG * NG), BF),
            pltpu.VMEM((16 * (NG * NG // LANES), LANES), F32),
            pltpu.VMEM((rows, cl), BF),
            pltpu.VMEM((rows, cl), F32),
            pltpu.VMEM(measured.shape, F32),
            pltpu.VMEM((steps, angles // 2) + measured.shape[1:], F32),
            pltpu.VMEM((steps, angles // 2) + measured.shape[1:], F32),
            pltpu.VMEM(measured.shape, F32),
            pltpu.VMEM((cl, rows), BF),
            pltpu.VMEM((n, cl, vt), F32),
            pltpu.VMEM((tiles, n, cl, vt), BF),
            pltpu.VMEM((tiles, n, cl, vt), BF),
            dma((4,)),
            dma((tiles, n)),
            dma((1,)),
            dma((1,)),
            dma((n,)),
            dma((n,)),
            dma((n, slabs)),
            dma((n, slabs)),
            dma((n, slabs, split)),
            dma((n, slabs, split)),
            dma((n, slabs, split)),
            dma((n, slabs, split)),
            dma((tiles, n)),
            dma((tiles, n)),
            dma((steps + 1,)),
            dma((steps + 1,)),
            dma((tiles, n)),
            dma((tiles, n)),
        ],
        compiler_params=pltpu.CompilerParams(
            collective_id=0, has_side_effects=True, vmem_limit_bytes=60 * 1024 * 1024),
        name="step",
    )(coefficients, measured, ray_voxels.reshape(rows, -1), ray_weights.reshape(rows, -1),
      angle_ids, angle_table, harmonics)
    chan_width = chans // n
    residual = lax.dynamic_slice_in_dim(residual, lax.axis_index("coef") * chan_width, chan_width, 3)
    return updated, residual


def solution(mesh):
    in_specs = (
        P("coef", ("groups", "slab")),
        P("groups", "slab", None, None),
        P(),
        P(),
        P(),
        P(None, "coef", None),
        P("coef", None),
    )
    out_specs = (P("coef", ("groups", "slab")), P("groups", "slab", None, "coef"))
    return jax.shard_map(body, mesh=mesh, in_specs=in_specs, out_specs=out_specs, check_vma=False)
```

```python
import functools

import jax
import jax.numpy as jnp
from jax import lax
from jax.experimental import pallas as pl
from jax.experimental.pallas import tpu as pltpu
from jax.sharding import PartitionSpec as P

NG = 64
LANES = 128
BF = jnp.bfloat16
F32 = jnp.float32
NT = (((1,), (1,)), ((), ()))
TN = (((0,), (0,)), ((), ()))
NN = (((1,), (0,)), ((), ()))


def dot(a, b, dims):
    return lax.dot_general(a, b, dims, preferred_element_type=F32)


def kernel(n, slabs, split, tiles, coef_hbm, meas_hbm, vox_ref, wgt_ref, ids_ref, table_hbm, harm_hbm,
           upd_hbm, resid_ref,
           coef, coef_bf, meas, table, harm, recv, matrix, prod, rays, ray_acc, part, half, half_bf, inbox, inbox_bf, full,
           bp_t, racc, rsend, rrecv,
           load_sem, coef_sem, out_sem, own_s, own_r, hx_s, hx_r, hz_s, hz_r, hy_s, hy_r, hs_s, hs_r,
           csend, crecv, psend, precv, gsend, grecv):
    me = lax.axis_index("coef")
    mz = lax.axis_index("slab")
    my = lax.axis_index("groups") if split > 1 else 0
    cl, width = coef.shape
    share = width // n
    vt = share // tiles
    angles, layers, nrays, chans = meas.shape
    plane = NG * NG
    orient = harm.shape[2]
    steps = n.bit_length() - 1
    sibling = me + 1 - 2 * lax.rem(me, 2)

    mates = [lax.rem(me + 2 * e, n) for e in range(1, n // 2)]
    sib_mates = [lax.rem(sibling + 2 * e, n) for e in range(1, n // 2)]
    targets = mates + sib_mates + [sibling]
    blocks = []
    for d, j in enumerate(targets + [me]):
        at = pl.ds(pl.multiple_of(j * share, LANES), share)
        blocks.append(pltpu.make_async_copy(coef_hbm.at[:, at], coef.at[:, at], coef_sem.at[d]))
    loads = [
        pltpu.make_async_copy(harm_hbm, harm.at[me], load_sem.at[0]),
        pltpu.make_async_copy(table_hbm, table, load_sem.at[1]),
        pltpu.make_async_copy(meas_hbm, meas, load_sem.at[2]),
    ]
    for item in blocks:
        item.start()
    for item in loads:
        item.start()

    barrier = pltpu.get_barrier_semaphore()
    for axis, index, size in (("coef", me, n), ("slab", mz, slabs), ("groups", my, split)):
        for d in range(1, size):
            pl.semaphore_signal(barrier, inc=1, device_id={axis: lax.rem(index + d, size)},
                                device_id_type=pl.DeviceIdType.MESH)
    pl.semaphore_wait(barrier, n + slabs + split - 3)

    def remote(src, dst, ssem, rsem, target, axis="coef"):
        return pltpu.make_async_remote_copy(
            src_ref=src, dst_ref=dst, send_sem=ssem, recv_sem=rsem,
            device_id={axis: target}, device_id_type=pl.DeviceIdType.MESH)

    ow = orient // (slabs * split)
    sent = []

    def cols(zi, yi):
        return pl.ds(pl.multiple_of((zi * split + yi) * ow, LANES), ow)

    def launch(*args):
        item = remote(*args)
        item.start()
        sent.append(item)

    def arrived(ref, sem):
        remote(ref, ref, sem, sem, sibling).wait_recv()

    def spread_y(b, zi):
        piece = harm.at[b, :, cols(zi, my)]
        for d in range(1, split):
            to = lax.rem(my + d, split)
            launch(piece, piece, hy_s.at[b, zi, to], hy_r.at[b, zi, my], to, "groups")

    def to_sibling(b, zi, yi):
        piece = harm.at[b, :, cols(zi, yi)]
        launch(piece, piece, hs_s.at[b, zi, yi], hs_r.at[b, zi, yi], sibling)

    for b in mates:
        launch(harm_hbm.at[:, cols(mz, my)], harm.at[me, :, cols(mz, my)], hx_s.at[b],
               hx_r.at[me], b)
    launch(harm_hbm, harm.at[me], own_s.at[0], own_r.at[0], sibling)

    def x_arrive():
        for b in mates:
            piece = harm.at[b, :, cols(mz, my)]
            arrived(piece, hx_r.at[b])
            for d in range(1, slabs):
                to = lax.rem(mz + d, slabs)
                launch(piece, piece, hz_s.at[b, to], hz_r.at[b, mz], to, "slab")
            spread_y(b, mz)
            to_sibling(b, mz, my)

    def z_arrive(d):
        zi = lax.rem(mz + d, slabs)
        for b in mates:
            arrived(harm.at[b, :, cols(zi, my)], hz_r.at[b, zi])
            spread_y(b, zi)
            to_sibling(b, zi, my)

    def y_arrive():
        for d in range(slabs):
            zi = lax.rem(mz + d, slabs)
            for b in mates:
                for f in range(1, split):
                    yi = lax.rem(my + f, split)
                    arrived(harm.at[b, :, cols(zi, yi)], hy_r.at[b, zi, yi])
                    to_sibling(b, zi, yi)

    def sibling_arrive():
        arrived(harm.at[sibling], own_r.at[0])
        for b in sib_mates:
            for zi in range(slabs):
                for yi in range(split):
                    arrived(harm.at[b, :, cols(zi, yi)], hs_r.at[b, zi, yi])

    coef_copies = []
    far = len(targets) - 1

    def span(j, t):
        return pl.ds(pl.multiple_of(j * share + t * vt, LANES), vt)

    def cast(d, t):
        j = (targets + [me])[d]
        if t == 0:
            blocks[d].wait()
        coef_bf[:, span(j, t)] = coef[:, span(j, t)].astype(BF)

    def send(d, t):
        j = targets[d]
        item = remote(coef_bf.at[:, span(j, t)], recv.at[t, me], csend.at[t, d], crecv.at[t, me], j)
        item.start()
        coef_copies.append(item)

    for d in range(far):
        cast(d, 0)
    for d in range(far):
        send(d, 0)
    cast(far, 0)
    for t in range(1, tiles):
        for d in range(far + 1):
            cast(d, t)
        for d in range(far):
            send(d, t)
    for t in range(tiles):
        send(far, t)
    for t in range(tiles):
        cast(far + 1, t)
        recv[t, me] = coef_bf[:, span(me, t)]

    samples = vox_ref.shape[1]
    rows_hi = plane // LANES
    pos_lo = lax.broadcasted_iota(jnp.int32, (LANES, samples), 0)
    pos_hi = lax.broadcasted_iota(jnp.int32, (rows_hi, samples), 0)

    def build(g, carry):
        r0 = pl.multiple_of(g * 16, 16)
        vox = vox_ref[pl.ds(r0, 16), :]
        wgt = wgt_ref[pl.ds(r0, 16), :].astype(F32) * (1.0 / 256.0)
        high = vox // LANES
        low = vox - high * LANES
        for i in range(16):
            oh_hi = jnp.where(high[i:i + 1, :] == pos_hi, wgt[i:i + 1, :], 0.0).astype(BF)
            oh_lo = jnp.where(low[i:i + 1, :] == pos_lo, 1.0, 0.0).astype(BF)
            prod[pl.ds(i * rows_hi, rows_hi), :] = dot(oh_hi, oh_lo, NT)
        for h in range(rows_hi):
            matrix[pl.ds(r0, 16), pl.ds(h * LANES, LANES)] = prod[
                pl.ds(h, 16, stride=rows_hi), :].astype(BF)
        return carry

    groups16 = (angles * nrays) // 16
    parts = 4
    for q in range(parts):
        lax.fori_loop(q * groups16 // parts, (q + 1) * groups16 // parts, build, 0)
        if q == 0:
            x_arrive()
        elif q < slabs:
            z_arrive(q)
    for q in range(parts, slabs):
        z_arrive(q)

    oc = 512
    back = []

    def penalty_tile(t):
        for d in range(1, n):
            j = lax.rem(me + d, n)
            arrived(recv.at[t, j], crecv.at[t, j])
        racc[...] = jnp.zeros_like(racc)

        def penalty(i, carry):
            at = pl.multiple_of(i * oc, oc)
            field = dot(harm[0, :, pl.ds(at, oc)], recv[t, 0], TN)
            for j in range(1, n):
                field += dot(harm[j, :, pl.ds(at, oc)], recv[t, j], TN)
            slope = (-1.0 / (1.0 + jnp.exp(field))).astype(BF)
            for j in range(n):
                racc[j] += dot(harm[j, :, pl.ds(at, oc)], slope, NN)
            return carry

        lax.fori_loop(0, orient // oc, penalty, 0)
        rsend[t] = racc[...].astype(BF)
        rrecv[t, me] = rsend[t, me]
        for d, j in enumerate(targets):
            item = remote(rsend.at[t, j], rrecv.at[t, me], gsend.at[t, d], grecv.at[t, me], j)
            item.start()
            back.append(item)

    early = 0
    for t in range(early):
        penalty_tile(t)

    kc = 512
    loads[1].wait()
    for z in range(layers):
        ray_acc[...] = jnp.zeros_like(ray_acc)

        def project(i, carry, z=z):
            at = pl.multiple_of(i * kc, kc)
            ray_acc[...] += dot(matrix[:, pl.ds(at, kc)],
                                coef_bf[:, pl.ds(pl.multiple_of(z * plane + i * kc, kc), kc)], NT)
            return carry

        lax.fori_loop(0, plane // kc, project, 0)
        rays[...] = ray_acc[...].astype(BF)
        for a in range(angles):
            part[a, z] = dot(rays[a * nrays:(a + 1) * nrays, :], table[ids_ref[a]], NN)

    ha = angles // 2
    par = lax.rem(me, 2)
    mine, other = pl.ds(par * ha, ha), pl.ds((1 - par) * ha, ha)

    def swap(s):
        if s == 0:
            return remote(part.at[other], inbox.at[0], psend.at[0], precv.at[0], sibling)
        if s == steps:
            return remote(half.at[s - 1], full.at[mine], psend.at[s], precv.at[s], sibling)
        bit = 1 << s
        partner = me + (1 - 2 * lax.rem(me // bit, 2)) * bit
        return remote(half_bf.at[s - 1], inbox_bf.at[s - 1], psend.at[s], precv.at[s], partner)

    swaps = [swap(s) for s in range(steps + 1)]
    swaps[0].start()

    def finish_swap(s):
        swaps[s].wait_recv()
        if s < steps:
            if s == 0:
                half[s] = part[mine] + inbox[0]
            else:
                half[s] = half[s - 1] + inbox_bf[s - 1].astype(F32)
            if s + 1 < steps:
                half_bf[s] = half[s].astype(BF)
            swaps[s + 1].start()

    loads[0].wait()
    y_arrive()
    finish_swap(0)
    sibling_arrive()

    done_swaps = 1
    for t in range(early, tiles):
        penalty_tile(t)
        if done_swaps < steps:
            finish_swap(done_swaps)
            done_swaps += 1
    while done_swaps <= steps:
        finish_swap(done_swaps)
        done_swaps += 1

    loads[2].wait()
    full[mine] = half[steps - 1]
    full[...] = full[...] - meas[...]
    cw = chans // n
    for c in range(n):
        @pl.when(me == c)
        def _(c=c):
            resid_ref[...] = full[:, :, :, c * cw:(c + 1) * cw]

    for z in range(layers):
        for a in range(angles):
            bp_t[:, a * nrays:(a + 1) * nrays] = dot(
                table[ids_ref[a]], full[a, z].astype(BF), NT).astype(BF)

        def gradient(i, carry, z=z):
            at = pl.multiple_of(i * kc, kc)
            to = pl.multiple_of(z * plane + i * kc, kc)
            coef[:, pl.ds(to, kc)] = coef[:, pl.ds(to, kc)] - 0.5 * dot(
                bp_t[...], matrix[:, pl.ds(at, kc)], NN)
            return carry

        lax.fori_loop(0, plane // kc, gradient, 0)

    outs = []
    for t in range(tiles):
        for d, j in enumerate([me] + targets):
            if j is not me:
                arrived(rrecv.at[t, j], grecv.at[t, j])
            coef[:, span(j, t)] = coef[:, span(j, t)] - 0.5 * rrecv[t, j].astype(F32)
            outs.append(pltpu.make_async_copy(coef.at[:, span(j, t)], upd_hbm.at[:, span(j, t)],
                                              out_sem.at[t, d]))
            outs[-1].start()
    for item in sent + coef_copies + back + swaps:
        item.wait_send()
    for item in outs:
        item.wait()


def body(coefficients, measured, ray_voxels, ray_weights, angle_ids, angle_table, harmonics):
    n = lax.axis_size("coef")
    slabs = lax.axis_size("slab")
    split = lax.axis_size("groups")
    if (harmonics.shape[1] // (slabs * split)) % LANES:
        split = 1
    cl, width = coefficients.shape
    angles, layers, nrays, chans = measured.shape
    rows = angles * nrays
    orient = harmonics.shape[1]
    share = width // n
    tiles = 2
    vt = share // tiles
    steps = n.bit_length() - 1
    any_spec = pl.BlockSpec(memory_space=pltpu.HBM)
    vmem_spec = pl.BlockSpec(memory_space=pltpu.VMEM)
    smem_spec = pl.BlockSpec(memory_space=pltpu.SMEM)
    dma = pltpu.SemaphoreType.DMA
    updated, residual = pl.pallas_call(
        functools.partial(kernel, n, slabs, split, tiles),
        out_shape=(jax.ShapeDtypeStruct(coefficients.shape, F32),
                   jax.ShapeDtypeStruct((angles, layers, nrays, chans // n), F32)),
        in_specs=[any_spec, any_spec, vmem_spec, vmem_spec, smem_spec, any_spec, any_spec],
        out_specs=(pl.BlockSpec(memory_space=pl.ANY), vmem_spec),
        scratch_shapes=[
            pltpu.VMEM((cl, width), F32),
            pltpu.VMEM((cl, width), BF),
            pltpu.VMEM(measured.shape, F32),
            pltpu.VMEM(angle_table.shape, BF),
            pltpu.VMEM((n, cl, orient), BF),
            pltpu.VMEM((tiles, n, cl, vt), BF),
            pltpu.VMEM((rows, NG * NG), BF),
            pltpu.VMEM((16 * (NG * NG // LANES), LANES), F32),
            pltpu.VMEM((rows, cl), BF),
            pltpu.VMEM((rows, cl), F32),
            pltpu.VMEM(measured.shape, F32),
            pltpu.VMEM((steps, angles // 2) + measured.shape[1:], F32),
            pltpu.VMEM((max(steps - 1, 1), angles // 2) + measured.shape[1:], BF),
            pltpu.VMEM((1, angles // 2) + measured.shape[1:], F32),
            pltpu.VMEM((max(steps - 1, 1), angles // 2) + measured.shape[1:], BF),
            pltpu.VMEM(measured.shape, F32),
            pltpu.VMEM((cl, rows), BF),
            pltpu.VMEM((n, cl, vt), F32),
            pltpu.VMEM((tiles, n, cl, vt), BF),
            pltpu.VMEM((tiles, n, cl, vt), BF),
            dma((3,)),
            dma((n,)),
            dma((tiles, n)),
            dma((1,)),
            dma((1,)),
            dma((n,)),
            dma((n,)),
            dma((n, slabs)),
            dma((n, slabs)),
            dma((n, slabs, split)),
            dma((n, slabs, split)),
            dma((n, slabs, split)),
            dma((n, slabs, split)),
            dma((tiles, n)),
            dma((tiles, n)),
            dma((steps + 1,)),
            dma((steps + 1,)),
            dma((tiles, n)),
            dma((tiles, n)),
        ],
        compiler_params=pltpu.CompilerParams(
            collective_id=0, has_side_effects=True, vmem_limit_bytes=60 * 1024 * 1024),
        name="step",
    )(coefficients, measured, ray_voxels.reshape(rows, -1), ray_weights.reshape(rows, -1),
      angle_ids, angle_table, harmonics)
    return updated, residual


def solution(mesh):
    in_specs = (
        P("coef", ("groups", "slab")),
        P("groups", "slab", None, None),
        P(),
        P(),
        P(),
        P(None, "coef", None),
        P("coef", None),
    )
    out_specs = (P("coef", ("groups", "slab")), P("groups", "slab", None, "coef"))
    return jax.shard_map(body, mesh=mesh, in_specs=in_specs, out_specs=out_specs, check_vma=False)
```
